512 devices in a mesh: grp: 16 (over z), mod: 32 (over x, y, core).
Axes of the slice: x: 4, y: 4, z: 16, core: 2. Of those that a mesh axis runs over, the one named last changes fastest.
Arguments:
- tokens: bfloat16 [1024, 64, 32, 128], P(('grp', 'mod')), may hold values from -3 to 3
- lengths: int32 [1024], P(('grp', 'mod')), may hold values from 1 to 64, 32768 in all
- module_order: int32 [32], replicated, may hold values from 0 to 31, each once
Outputs:
- preconditioned: float32 [32, 1024, 4096], P('mod', 'grp')
The draws below stay inside these ranges and needn't reach their ends.
Inputs may be any that keep to these rules, and one draw needn't show every extreme that they name: `lengths`: each example's live tokens are its first slots; some example has exactly 64. `module_order`: each module appears exactly once.
All inputs are finite; a program needn't handle non-finite values. No bound on the sum of `lengths` on one device may be relied on, other than what follows from the above.
Results may differ from the reference program's by a relative error of at most 0.0068.
Values may be sent and summed in bfloat16 or wider, within the bound.
A program may use at most 64 MiB of HBM per device.

```python
import math
import jax
import jax.numpy as jnp
import numpy as np
from jax import lax

PROJ = 64
LEN = 64
ITERS = 3
MODULES = 32
EX_GRP = 64
EXAMPLES = 1024
N_GRP = 16


def steps_of(key, shape, cuts, low, largest):
    gain = 1.0
    for position, shards_of in cuts:
        steps = jax.random.uniform(jax.random.fold_in(jax.random.fold_in(key, 6), position), (shards_of,), jnp.float32, low / len(cuts), largest / len(cuts))
        gain = gain * jnp.repeat(jnp.exp(steps), shape[position] // shards_of).reshape((-1,) + (1,) * (len(shape) - 1 - position))
    return gain


def profile(amount, total, limit, skew):
    portions = [(1 << 20) // math.isqrt(grade ** skew) + 1 for grade in range(2, amount + 1)]
    surplus, counts = total - limit - (amount - 1), [1] * (amount - 1)
    while surplus > 0:
        movable = [i for i in range(amount - 1) if counts[i] < limit]
        whole, budget = sum([portions[i] for i in movable]), surplus
        for i in movable:
            addition = min(limit - counts[i], max(1, budget * portions[i] // whole), surplus)
            counts[i] = counts[i] + addition
            surplus = surplus - addition
    return np.array([limit] + counts)


def uneven_parts(stream_key, count, total, most, slope):
    if count == 2:
        one = jax.random.randint(stream_key, (), max(1, total - most), min(most, total - 1) + 1)
        return jnp.stack([one, total - one])
    tallies = jnp.asarray(profile(count, total, most, slope), jnp.int32)
    twos = (count - 1) // 2
    donor, sink = tallies[1:1 + 2 * twos:2], tallies[2:2 + 2 * twos:2]
    room = jnp.minimum(donor - 1, most - sink)
    shifted = jax.random.randint(jax.random.fold_in(stream_key, 1), (twos,), 0, 1 << 20) % (room + 1)
    tallies = tallies.at[1:1 + 2 * twos:2].set(donor - shifted).at[2:2 + 2 * twos:2].set(sink + shifted)
    return tallies[jax.random.permutation(jax.random.fold_in(stream_key, 2), count)]


def centred(rng, shape, spread, bound, cuts=(), held_as=jnp.bfloat16):
    result = jax.random.normal(rng, shape, jnp.float32) * spread
    if len(cuts) > 0:
        result = steps_of(rng, shape, cuts, -0.22, 0.18) * result
    return jnp.clip(result, min=-bound, max=bound).astype(held_as)


def setup_inputs(seed: int = 0) -> dict:
    streams_of = jax.random.split(jax.random.key(seed), 4)
    return {
        "tokens": centred(streams_of[0], (EXAMPLES, LEN, MODULES, 2 * PROJ), 0.5, 3.0, ((0, 512),)),
        "lengths": uneven_parts(streams_of[1], EXAMPLES, EXAMPLES * LEN // 2, LEN, 1).astype(jnp.int32),
        "module_order": jax.random.permutation(streams_of[2], MODULES).astype(jnp.int32),
    }


def start_basis(row_count, col_count):
    row_index = jnp.arange(row_count, dtype=jnp.float32)[:, None] + 0.5
    col_index = jnp.arange(col_count, dtype=jnp.float32)[None, :] + 0.5
    return jnp.cos(jnp.pi * row_index * col_index / row_count)

def orthonormal(matrix):
    for repeat in range(2):
        cross_gram = jnp.dot(matrix.T, matrix, precision=lax.Precision.HIGHEST)
        factor = jnp.linalg.cholesky(cross_gram)
        matrix = jax.scipy.linalg.solve_triangular(factor, matrix.T, lower=True).T
    return matrix

def merge_pair(lower_sketch, upper_sketch):
    stacked = jnp.concatenate([lower_sketch, upper_sketch], axis=0)
    kernel = jnp.dot(stacked, stacked.T, precision=lax.Precision.HIGHEST)
    current = start_basis(stacked.shape[0], lower_sketch.shape[0])
    for repeat in range(ITERS):
        current = orthonormal(jnp.dot(kernel, current, precision=lax.Precision.HIGHEST))
    return jnp.dot(current.T, stacked, precision=lax.Precision.HIGHEST)

def precondition(group_rows, sketch):
    sketch_rows = sketch.shape[0]
    damping = 0.1 * jnp.sum(sketch * sketch) / sketch_rows + 1e-06
    capacitance = jnp.dot(sketch, sketch.T, precision=lax.Precision.HIGHEST) + damping * jnp.eye(sketch_rows, dtype=jnp.float32)
    projected = jnp.dot(group_rows, sketch.T, precision=lax.Precision.HIGHEST)
    factor = jnp.linalg.cholesky(capacitance)
    middle = jax.scipy.linalg.solve_triangular(factor, projected.T, lower=True)
    weights = jax.scipy.linalg.solve_triangular(factor, middle, lower=True, trans=1).T
    return group_rows - jnp.dot(weights, sketch, precision=lax.Precision.HIGHEST)

def module_features(picked, lengths):
    half_width = picked.shape[-1] // 2
    live_mask = jnp.arange(picked.shape[1], dtype=jnp.int32)[None, :] < lengths[:, None]
    grad_side = jnp.where(live_mask[:, :, None], picked[:, :, half_width:], jnp.zeros((), picked.dtype))
    input_side = picked[:, :, :half_width]
    outer = jnp.einsum('eto,eti->eoi', grad_side.astype(jnp.float32), input_side.astype(jnp.float32))
    return outer.reshape(picked.shape[0], half_width * half_width).astype(jnp.bfloat16)

def reference(tokens, lengths, module_order):
    levels = N_GRP.bit_length() - 1

    def one_module(slot):
        picked = lax.dynamic_index_in_dim(tokens, module_order[slot], axis=2, keepdims=False)
        leaves = module_features(picked, lengths).astype(jnp.float32)
        sketches = leaves.reshape(N_GRP, EX_GRP, leaves.shape[-1])
        for height in range(levels):
            sketches = jax.vmap(merge_pair)(sketches[0::2], sketches[1::2])
        return precondition(leaves, sketches[0])
    return lax.map(one_module, jnp.arange(MODULES, dtype=jnp.int32))
```

```python
import functools

import jax
import jax.numpy as jnp
import numpy as np
from jax import lax
from jax.experimental import pallas as pl
from jax.experimental.pallas import tpu as pltpu
from jax.sharding import PartitionSpec as P

ITERS = 3
F32 = jnp.float32
BF16 = jnp.bfloat16
EXACT = lax.Precision.HIGHEST
VMEM = pltpu.MemorySpace.VMEM
SMEM = pltpu.MemorySpace.SMEM


def start_rows(row_count, col_count):
    row_index = np.arange(row_count, dtype=np.float64)[None, :] + 0.5
    col_index = np.arange(col_count, dtype=np.float64)[:, None] + 0.5
    return np.cos(np.pi * row_index * col_index / row_count).astype(np.float32)


def mm(a, b):
    return lax.dot_general(a, b, (((1,), (0,)), ((), ())), precision=EXACT, preferred_element_type=F32)


def mm_nt(a, b):
    return lax.dot_general(a, b, (((1,), (1,)), ((), ())), precision=EXACT, preferred_element_type=F32)


def bmm(a, b):
    return lax.dot_general(a, b, (((1,), (0,)), ((), ())), preferred_element_type=F32)


def bmm_nt(a, b):
    return lax.dot_general(a, b, (((1,), (1,)), ((), ())), preferred_element_type=F32)


def split2(x):
    hi = x.astype(BF16)
    return hi, (x - hi.astype(F32)).astype(BF16)


def split3(x):
    hi, rest = x.astype(BF16), None
    rest = x - hi.astype(F32)
    mid = rest.astype(BF16)
    return hi, mid, (rest - mid.astype(F32)).astype(BF16)


def eliminate(gram, rows):
    size = gram.shape[0]
    blocks = size // 8
    sub = lax.broadcasted_iota(jnp.int32, (8, 128), 0)
    padded = jnp.concatenate([gram, jnp.zeros((size, 128 - size), F32)], axis=1)
    left = [padded[8 * i : 8 * i + 8] for i in range(blocks)]
    right = [rows[8 * i : 8 * i + 8] for i in range(blocks)]

    def along_lanes(x, lane):
        return jnp.broadcast_to(x[:, lane : lane + 1], (8, 128))

    def along_rows(x, row):
        return jnp.broadcast_to(x[row : row + 1, :], (8, 128))

    done = []
    for k in range(blocks):
        p_left, p_right = left[k], right[k]
        cols = [along_lanes(p_left, 8 * k + c) for c in range(8)]
        below = {i: [along_lanes(left[i], 8 * k + c) for c in range(8)] for i in range(k + 1, blocks)}
        pivots = jnp.ones((8, 128), F32)
        reduced = jnp.zeros((8, 128), F32)
        for j in range(8):
            col = cols[j]
            pivot = along_rows(col, j)
            inverse = 1.0 / pivot
            here = sub == j
            pivots = jnp.where(here, pivot, pivots)
            row_right = along_rows(p_right, j)
            reduced = jnp.where(here, row_right, reduced)
            for c in range(j + 1, 8):
                scaled = along_rows(cols[c], j) * inverse
                cols[c] = jnp.where(here, scaled, cols[c] - col * scaled)
            scaled = along_rows(p_left, j) * inverse
            p_left = jnp.where(here, scaled, p_left - col * scaled)
            scaled = row_right * inverse
            p_right = jnp.where(here, scaled, p_right - col * scaled)
        done.append(reduced * lax.rsqrt(pivots))
        for c in range(8):
            row_left, row_right = along_rows(p_left, c), along_rows(p_right, c)
            for i in range(k + 1, blocks):
                left[i] = left[i] - below[i][c] * row_left
                right[i] = right[i] - below[i][c] * row_right
    return jnp.concatenate(done, axis=0)


def basis_of(kernel, start):
    def step(_, basis):
        image = mm(basis, kernel)
        return eliminate(mm_nt(image, image), image)

    basis = lax.fori_loop(0, ITERS, step, start)
    gram = mm_nt(basis, basis)
    row = lax.broadcasted_iota(jnp.int32, gram.shape, 0)
    col = lax.broadcasted_iota(jnp.int32, gram.shape, 1)
    fix = jnp.where(row > col, gram, 0.0) + jnp.where(row == col, 0.5 * (gram - 1.0), 0.0)
    basis = basis - mm(fix, basis)
    return basis, mm_nt(mm(basis, kernel), basis)


def pack(x):
    return jnp.concatenate([x[:32], x[32:]], axis=1)


def unpack(x):
    return jnp.concatenate([x[:, :64], x[:, 64:]], axis=0)


def assemble(lower, cross, upper):
    top = jnp.concatenate([lower, cross], axis=1)
    return jnp.concatenate([top, jnp.concatenate([cross.T, upper], axis=1)], axis=0)


def split_basis(basis):
    hi, lo = split2(basis)
    zero = jnp.zeros((64, 64), BF16)
    top = jnp.concatenate([hi[:, :64], hi[:, :64], hi[:, 64:], hi[:, 64:]], axis=1)
    low = jnp.concatenate([lo[:, :64], zero, lo[:, 64:], zero], axis=1)
    return jnp.concatenate([top, low], axis=0)


def feature_kernel(lengths, order, tokens, out):
    def one(slot, carry):
        module = order[slot]
        for example in range(2):
            x = tokens[module, example]
            live = lax.broadcasted_iota(jnp.int32, x.shape, 0) < lengths[example]
            x = jnp.where(live, x.astype(F32), 0.0).astype(BF16)
            outer = lax.dot_general(x, x, (((0,), (0,)), ((), ())), preferred_element_type=F32)
            both = jnp.concatenate([outer[64:96, :64], outer[96:, :64]], axis=1)
            out[slot, example] = both.astype(BF16)
        return carry

    lax.fori_loop(0, 32, one, 0)


def tree_kernel(
    leaf, start, out,
    pair, quad, slab1, slab2, slab3, send2,
    d0_out, d0_in, qd_out, qd_in, d2_out, d2_in,
    x0, x1, x2,
    bulk_send, bulk_recv, small_send, small_recv,
    x0_send, x0_recv, x1_send, x1_recv, x2_send, x2_recv,
    right_send, right_recv, left_send, left_recv,
):
    me = lax.axis_index("grp")
    b0, b1, b2 = me % 2, (me // 2) % 2, (me // 4) % 2
    sister0 = me + 1 - 2 * b0
    sister1 = me + 2 - 4 * b1
    sister2 = me + 4 - 8 * b2

    def to(index):
        return dict(device_id={"grp": index}, device_id_type=pl.DeviceIdType.MESH)

    def send(src, dst, sems, recvs, slot_send, slot_recv, index):
        copy = pltpu.make_async_remote_copy(
            src_ref=src, dst_ref=dst, send_sem=sems.at[slot_send], recv_sem=recvs.at[slot_recv], **to(index)
        )
        copy.start()
        return copy

    barrier = pltpu.get_barrier_semaphore()
    for d in range(1, 16):
        pl.semaphore_signal(barrier, inc=1, **to((me + d) % 16))
    pl.semaphore_wait(barrier, 15)

    leaf_copy = send(
        leaf.at[pl.ds((1 - b0) * 16, 16)], pair.at[:, pl.ds(b0 * 64, 64), :],
        bulk_send, bulk_recv, 0, 0, sister0,
    )

    def own_gram(r, acc):
        slab = leaf[r]
        return acc + bmm_nt(slab, slab)

    d_own = lax.fori_loop(0, 32, own_gram, jnp.zeros((64, 64), F32), unroll=8)
    d0_out[...] = pack(d_own)
    d_copy = send(d0_out, d0_in, small_send, small_recv, 0, 0, sister0)
    pair[:, pl.ds(b0 * 64, 64), :] = leaf[pl.ds(b0 * 16, 16)]

    early = []
    for other in range(2):
        target = sister1 - b0 + other
        offset = other * 16 + (1 - b1) * 8
        early.append((
            leaf.at[pl.ds(offset, 8)], quad.at[:, pl.ds(b0 * 64, 64), :],
            bulk_send, bulk_recv, 1 + other, 1 + b0, target,
        ))
    leaf_copy.wait()
    early = [send(*args) for args in early]
    d_copy.wait()

    def reduce_cross(partial, box, sems, recvs, members):
        mine = me % members
        base = me - mine
        box[mine] = pack(partial)
        copies = [
            send(box.at[mine], box.at[mine], sems, recvs, d, mine, base + (mine + d) % members)
            for d in range(1, members)
        ]
        for copy in copies:
            copy.wait_send()
        for d in range(1, members):
            source = (mine + d) % members
            pltpu.make_async_remote_copy(
                src_ref=box.at[source], dst_ref=box.at[source], send_sem=sems.at[d],
                recv_sem=recvs.at[source], **to(base + source)
            ).wait_recv()
        total = box[0]
        for i in range(1, members):
            total = total + box[i]
        return unpack(total)

    def cross0(r, acc):
        slab = pair[r]
        return acc + bmm_nt(slab[:64], slab[64:])

    cross = lax.fori_loop(0, 16, cross0, jnp.zeros((64, 64), F32), unroll=8)
    cross = reduce_cross(cross, x0, x0_send, x0_recv, 2)
    d_sister = unpack(d0_in[...])
    kernel = assemble(jnp.where(b0 == 0, d_own, d_sister), cross, jnp.where(b0 == 0, d_sister, d_own))
    basis, d_own = basis_of(kernel, start[...])
    qd_out[:64] = basis
    qd_out[64:] = pack(d_own)
    qd_copy = send(qd_out, qd_in, small_send, small_recv, 1, 1, sister1)

    def merged0(b, slabs, first, side):
        operand = jnp.concatenate(split3(b), axis=0)

        def one(r, carry):
            product = bmm(operand, slabs[first + r])
            product = product[:64] + product[64:128] + product[128:]
            hi, lo = split2(product)
            slab1[r, pl.ds(side * 128, 64), :] = hi
            slab1[r, pl.ds(side * 128 + 64, 64), :] = lo
            return carry

        lax.fori_loop(0, 8, one, 0, unroll=4)

    merged0(basis, pair, b1 * 8, b1)
    for copy in early:
        copy.wait_send()
    for other in range(2):
        pltpu.make_async_remote_copy(
            src_ref=leaf.at[pl.ds(0, 8)], dst_ref=quad.at[:, pl.ds(other * 64, 64), :],
            send_sem=bulk_send.at[1 + other], recv_sem=bulk_recv.at[1 + other], **to(sister1 - b0 + other)
        ).wait_recv()
    qd_copy.wait()
    merged0(qd_in[:64], quad, 0, 1 - b1)
    d_sister = unpack(qd_in[64:])

    def cross_of(slabs, count):
        def one(r, acc):
            slab = slabs[r]
            return acc + bmm_nt(slab[:128], slab[128:])

        acc = lax.fori_loop(0, count, one, jnp.zeros((128, 128), F32), unroll=4)
        return acc[:64, :64] + acc[:64, 64:] + acc[64:, :64] + acc[64:, 64:]

    cross = reduce_cross(cross_of(slab1, 8), x1, x1_send, x1_recv, 4)
    kernel = assemble(jnp.where(b1 == 0, d_own, d_sister), cross, jnp.where(b1 == 0, d_sister, d_own))
    basis, d_own = basis_of(kernel, start[...])
    d2_out[...] = pack(d_own)
    d_copy = send(d2_out, d2_in, small_send, small_recv, 2, 2, sister2)

    def merged(operand, slab):
        product = bmm(operand, slab)
        return product[:64] + product[64:]

    operand = split_basis(basis)
    for r in range(4):
        hi, lo = split2(merged(operand, slab1[(1 - b2) * 4 + r]))
        send2[r, :64] = hi
        send2[r, 64:] = lo
    slab_copy = send(send2, slab2.at[:, pl.ds(b2 * 128, 128), :], bulk_send, bulk_recv, 3, 3, sister2)
    for r in range(4):
        hi, lo = split2(merged(operand, slab1[b2 * 4 + r]))
        slab2[r, pl.ds(b2 * 128, 64), :] = hi
        slab2[r, pl.ds(b2 * 128 + 64, 64), :] = lo
    slab_copy.wait()
    d_copy.wait()
    d_sister = unpack(d2_in[...])
    cross = reduce_cross(cross_of(slab2, 4), x2, x2_send, x2_recv, 8)
    kernel = assemble(jnp.where(b2 == 0, d_own, d_sister), cross, jnp.where(b2 == 0, d_sister, d_own))
    basis, _ = basis_of(kernel, start[...])

    operand = split_basis(basis)
    column, side = me % 8, me // 8
    for r in range(4):
        hi, lo = split2(merged(operand, slab2[r]))
        slab3[column, r, pl.ds(side * 128, 64), :] = hi
        slab3[column, r, pl.ds(side * 128 + 64, 64), :] = lo

    right, left = (me + 1) % 16, (me + 15) % 16

    def part(index, half):
        index = index % 16
        return slab3.at[index % 8, pl.ds(half * 2, 2), pl.ds(index // 8 * 128, 128), :]

    def hop(step, half, rightward):
        origin = me + 16 - (step - 1) if rightward else me + (step - 1)
        sems, recvs = (right_send, right_recv) if rightward else (left_send, left_recv)
        slot = (step - 1) * 2 + half
        ref = part(origin, half)
        return pltpu.make_async_remote_copy(
            src_ref=ref, dst_ref=ref, send_sem=sems.at[slot], recv_sem=recvs.at[slot],
            **to(right if rightward else left)
        )

    def landed(step, half, rightward):
        origin = me + 16 - step if rightward else me + step
        sems, recvs = (right_send, right_recv) if rightward else (left_send, left_recv)
        slot = (step - 1) * 2 + half
        ref = part(origin, half)
        return pltpu.make_async_remote_copy(
            src_ref=ref, dst_ref=ref, send_sem=sems.at[slot], recv_sem=recvs.at[slot],
            **to(right if rightward else left)
        )

    def travels(step, half, rightward):
        return step < 8 or (half == 0) == rightward

    for step in range(1, 9):
        for half in range(2):
            for rightward in (True, False):
                if step > 1 and travels(step - 1, half, rightward):
                    landed(step - 1, half, rightward).wait_recv()
                if travels(step, half, rightward):
                    hop(step, half, rightward).start()
    landed(8, 0, True).wait_recv()
    landed(8, 1, False).wait_recv()
    for step in range(1, 9):
        for half in range(2):
            for rightward in (True, False):
                if travels(step, half, rightward):
                    hop(step, half, rightward).wait_send()

    def first_row(c):
        return (c % 2) * 16 + (c // 2 % 2) * 8 + (c // 4) * 4

    def grams(c, carry):
        gram, along = carry
        for r in range(4):
            slab = slab3[c, r]
            gram = gram + bmm_nt(slab, slab)
            along = along + bmm_nt(leaf[first_row(c) + r], slab)
        return gram, along

    gram, along = lax.fori_loop(
        0, 8, grams, (jnp.zeros((256, 256), F32), jnp.zeros((64, 256), F32))
    )
    gram = jnp.concatenate([gram[:64] + gram[64:128], gram[128:192] + gram[192:]], axis=0)
    kernel = jnp.concatenate(
        [gram[:, :64] + gram[:, 64:128], gram[:, 128:192] + gram[:, 192:]], axis=1
    )
    along = jnp.concatenate(
        [along[:, :64] + along[:, 64:128], along[:, 128:192] + along[:, 192:]], axis=1
    )
    basis, d_final = basis_of(kernel, start[...])

    row = lax.broadcasted_iota(jnp.int32, (64, 64), 0)
    col = lax.broadcasted_iota(jnp.int32, (64, 64), 1)
    eye = jnp.where(row == col, 1.0, 0.0)
    damping = 0.1 * jnp.sum(d_final * eye, keepdims=True) / 64 + 1e-06
    capacitance = d_final + damping * eye
    inverse = eliminate(capacitance, jnp.concatenate([eye, jnp.zeros((64, 64), F32)], axis=1))[:, :64]
    projected = mm_nt(along, basis)
    weights = mm(mm_nt(projected, inverse), inverse)
    operand = split_basis(mm(weights, basis))

    def finish(c, carry):
        first = first_row(c)
        for r in range(0, 4, 2):
            one = leaf[first + r].astype(F32) - merged(operand, slab3[c, r])
            two = leaf[first + r + 1].astype(F32) - merged(operand, slab3[c, r + 1])
            where = (first + r) // 2
            out[:, pl.ds(pl.multiple_of(where * 128, 128), 128)] = jnp.concatenate([one[:, :64], two[:, :64]], axis=1)
            out[:, pl.ds(pl.multiple_of((where + 16) * 128, 128), 128)] = jnp.concatenate([one[:, 64:], two[:, 64:]], axis=1)
        return carry

    lax.fori_loop(0, 8, finish, 0)


def per_device(tokens, lengths, module_order):
    by_module = jnp.transpose(tokens, (2, 0, 1, 3))
    features = pl.pallas_call(
        feature_kernel,
        out_shape=jax.ShapeDtypeStruct((32, 2, 32, 128), BF16),
        in_specs=[pl.BlockSpec(memory_space=SMEM)] * 2 + [pl.BlockSpec(memory_space=VMEM)],
        out_specs=pl.BlockSpec(memory_space=VMEM),
        name="features",
    )(lengths, module_order, by_module)
    rows = lax.all_to_all(features, "mod", split_axis=0, concat_axis=0, tiled=True)
    leaf = jnp.transpose(rows.reshape(64, 32, 128), (1, 0, 2))
    dma = pltpu.SemaphoreType.DMA
    result = pl.pallas_call(
        tree_kernel,
        out_shape=jax.ShapeDtypeStruct((64, 4096), F32),
        in_specs=[pl.BlockSpec(memory_space=VMEM)] * 2,
        out_specs=pl.BlockSpec(memory_space=VMEM),
        scratch_shapes=[
            pltpu.VMEM((16, 128, 128), BF16),
            pltpu.VMEM((8, 128, 128), BF16),
            pltpu.VMEM((8, 256, 128), BF16),
            pltpu.VMEM((4, 256, 128), BF16),
            pltpu.VMEM((8, 4, 256, 128), BF16),
            pltpu.VMEM((4, 128, 128), BF16),
            pltpu.VMEM((32, 128), F32),
            pltpu.VMEM((32, 128), F32),
            pltpu.VMEM((96, 128), F32),
            pltpu.VMEM((96, 128), F32),
            pltpu.VMEM((32, 128), F32),
            pltpu.VMEM((32, 128), F32),
            pltpu.VMEM((2, 32, 128), F32),
            pltpu.VMEM((4, 32, 128), F32),
            pltpu.VMEM((8, 32, 128), F32),
            dma((4,)), dma((4,)), dma((3,)), dma((3,)),
            dma((2,)), dma((2,)), dma((4,)), dma((4,)), dma((8,)), dma((8,)),
            dma((16,)), dma((16,)), dma((16,)), dma((16,)),
        ],
        compiler_params=pltpu.CompilerParams(collective_id=0, has_side_effects=True),
        name="tree",
    )(leaf, jnp.asarray(start_rows(128, 64)))
    return result[None]


def solution(mesh):
    return jax.shard_map(
        per_device,
        mesh=mesh,
        in_specs=(P(("grp", "mod"), None, None, None), P(("grp", "mod")), P()),
        out_specs=P("mod", "grp", None),
        check_vma=False,
    )
```

```python
import functools

import jax
import jax.numpy as jnp
import numpy as np
from jax import lax
from jax.experimental import pallas as pl
from jax.experimental.pallas import tpu as pltpu
from jax.sharding import PartitionSpec as P

ITERS = 3
F32 = jnp.float32
BF16 = jnp.bfloat16
EXACT = lax.Precision.HIGHEST
VMEM = pltpu.MemorySpace.VMEM
SMEM = pltpu.MemorySpace.SMEM


def start_rows(row_count, col_count):
    row_index = np.arange(row_count, dtype=np.float64)[None, :] + 0.5
    col_index = np.arange(col_count, dtype=np.float64)[:, None] + 0.5
    return np.cos(np.pi * row_index * col_index / row_count).astype(np.float32)


def mm(a, b):
    return lax.dot_general(a, b, (((1,), (0,)), ((), ())), precision=EXACT, preferred_element_type=F32)


def mm_nt(a, b):
    return lax.dot_general(a, b, (((1,), (1,)), ((), ())), precision=EXACT, preferred_element_type=F32)


def bmm(a, b):
    return lax.dot_general(a, b, (((1,), (0,)), ((), ())), preferred_element_type=F32)


def bmm_nt(a, b):
    return lax.dot_general(a, b, (((1,), (1,)), ((), ())), preferred_element_type=F32)


def split2(x):
    hi = x.astype(BF16)
    return hi, (x - hi.astype(F32)).astype(BF16)


def split3(x):
    hi, rest = x.astype(BF16), None
    rest = x - hi.astype(F32)
    mid = rest.astype(BF16)
    return hi, mid, (rest - mid.astype(F32)).astype(BF16)


def eliminate(gram, rows):
    size = gram.shape[0]
    blocks = size // 8
    sub = lax.broadcasted_iota(jnp.int32, (8, 128), 0)
    padded = jnp.concatenate([gram, jnp.zeros((size, 128 - size), F32)], axis=1)
    left = [padded[8 * i : 8 * i + 8] for i in range(blocks)]
    right = [rows[8 * i : 8 * i + 8] for i in range(blocks)]

    def along_lanes(x, lane):
        return jnp.broadcast_to(x[:, lane : lane + 1], (8, 128))

    def along_rows(x, row):
        return jnp.broadcast_to(x[row : row + 1, :], (8, 128))

    done = []
    for k in range(blocks):
        p_left, p_right = left[k], right[k]
        cols = [along_lanes(p_left, 8 * k + c) for c in range(8)]
        below = {i: [along_lanes(left[i], 8 * k + c) for c in range(8)] for i in range(k + 1, blocks)}
        pivots = jnp.ones((8, 128), F32)
        reduced = jnp.zeros((8, 128), F32)
        for j in range(8):
            col = cols[j]
            pivot = along_rows(col, j)
            inverse = 1.0 / pivot
            here = sub == j
            pivots = jnp.where(here, pivot, pivots)
            row_right = along_rows(p_right, j)
            reduced = jnp.where(here, row_right, reduced)
            for c in range(j + 1, 8):
                scaled = along_rows(cols[c], j) * inverse
                cols[c] = jnp.where(here, scaled, cols[c] - col * scaled)
            scaled = along_rows(p_left, j) * inverse
            p_left = jnp.where(here, scaled, p_left - col * scaled)
            scaled = row_right * inverse
            p_right = jnp.where(here, scaled, p_right - col * scaled)
        done.append(reduced * lax.rsqrt(pivots))
        for c in range(8):
            row_left, row_right = along_rows(p_left, c), along_rows(p_right, c)
            for i in range(k + 1, blocks):
                left[i] = left[i] - below[i][c] * row_left
                right[i] = right[i] - below[i][c] * row_right
    return jnp.concatenate(done, axis=0)


def basis_of(kernel, start):
    def step(_, basis):
        image = mm(basis, kernel)
        return eliminate(mm_nt(image, image), image)

    basis = lax.fori_loop(0, ITERS, step, start)
    return basis, mm_nt(mm(basis, kernel), basis)


def pack(x):
    return jnp.concatenate([x[:32], x[32:]], axis=1)


def unpack(x):
    return jnp.concatenate([x[:, :64], x[:, 64:]], axis=0)


def assemble(lower, cross, upper):
    top = jnp.concatenate([lower, cross], axis=1)
    return jnp.concatenate([top, jnp.concatenate([cross.T, upper], axis=1)], axis=0)


def split_basis(basis):
    hi, lo = split2(basis)
    zero = jnp.zeros((64, 64), BF16)
    top = jnp.concatenate([hi[:, :64], hi[:, :64], hi[:, 64:], hi[:, 64:]], axis=1)
    low = jnp.concatenate([lo[:, :64], zero, lo[:, 64:], zero], axis=1)
    return jnp.concatenate([top, low], axis=0)


def features_of(x, live):
    zero = jnp.zeros((), x.dtype)
    x = jnp.where(live, x, zero)
    gradient = x.T[64:]
    lane = lax.broadcasted_iota(jnp.int32, gradient.shape, 1)
    sides = jnp.concatenate([jnp.where(lane < 64, gradient, zero), jnp.where(lane >= 64, gradient, zero)], axis=0)
    outer = bmm(sides, x)
    return [
        jnp.concatenate([outer[first : first + 32, :64], outer[first + 32 : first + 64, :64]], axis=1).astype(BF16)
        for first in (0, 64)
    ]


class Ring:
    def __init__(self, me, slabs, sems, to):
        self.me, self.slabs, self.to = me, slabs, to
        self.sems = {True: sems[:2], False: sems[2:]}

    def copy(self, step, part, rightward, arriving):
        behind = step if arriving else step - 1
        origin = (self.me + 16 - behind if rightward else self.me + behind) % 16
        ref = self.slabs.at[origin % 8, part, pl.ds(origin // 8 * 128, 128), :]
        send, recv = self.sems[rightward]
        slot = (step - 1) * 4 + part
        return pltpu.make_async_remote_copy(
            src_ref=ref, dst_ref=ref, send_sem=send.at[slot], recv_sem=recv.at[slot],
            **self.to((self.me + (1 if rightward else 15)) % 16)
        )

    @staticmethod
    def travels(step, part, rightward):
        return step < 8 or (part < 2) == rightward

    def advance(self, step):
        for part in range(4):
            for rightward in (True, False):
                if step > 1 and self.travels(step - 1, part, rightward):
                    self.copy(step - 1, part, rightward, True).wait_recv()
                if step < 9 and self.travels(step, part, rightward):
                    self.copy(step, part, rightward, False).start()

    def drain(self):
        for step in range(1, 9):
            for part in range(4):
                for rightward in (True, False):
                    if self.travels(step, part, rightward):
                        self.copy(step, part, rightward, False).wait_send()


def tree_kernel(
    lengths, order, tokens, start, out,
    by_module, features, rows, leaf,
    pair, quad, slab1, slab2, slab3, send2h, send2l, along,
    d0_out, d0_in, qd_out, qd_in, d2_out, d2_in,
    x0, x1, x2, wide,
    to_owner, at_owner,
    bulk_send, bulk_recv, small_send, small_recv,
    x0_send, x0_recv, x1_send, x1_recv, x2_send, x2_recv,
    *ring_sems,
):
    me, owner = lax.axis_index("grp"), lax.axis_index("mod")
    b0, b1, b2 = me % 2, (me // 2) % 2, (me // 4) % 2
    sister0 = me + 1 - 2 * b0
    sister1 = me + 2 - 4 * b1
    sister2 = me + 4 - 8 * b2

    def to(index):
        return dict(device_id={"grp": index}, device_id_type=pl.DeviceIdType.MESH)

    def across(index):
        return dict(device_id={"mod": index}, device_id_type=pl.DeviceIdType.MESH)

    def send(src, dst, sems, recvs, slot_send, slot_recv, index):
        copy = pltpu.make_async_remote_copy(
            src_ref=src, dst_ref=dst, send_sem=sems.at[slot_send], recv_sem=recvs.at[slot_recv], **to(index)
        )
        copy.start()
        return copy

    barrier = pltpu.get_barrier_semaphore()

    def greet(d, carry):
        pl.semaphore_signal(barrier, inc=1, **across((owner + d) % 32))
        return carry

    lax.fori_loop(1, 32, greet, 0)
    for d in range(1, 8):
        pl.semaphore_signal(barrier, inc=1, **to(me // 8 * 8 + (me + d) % 8))
    pl.semaphore_signal(barrier, inc=1, **to((me + 1) % 16))
    pl.semaphore_signal(barrier, inc=1, **to((me + 15) % 16))

    for example in range(2):
        by_module[:, pl.ds(example * 64, 64), :] = jnp.transpose(tokens[example], (1, 0, 2))
    token = lax.broadcasted_iota(jnp.int32, (128, 128), 0)
    live = token < jnp.where(token < 64, lengths[0], 64 + lengths[1])

    def make(group, carry):
        for i in range(16):
            slot = group * 16 + i
            first, second = features_of(by_module[order[slot]], live)
            features[slot, 0] = first
            features[slot, 1] = second
        return carry

    lax.fori_loop(0, 2, make, 0)
    pl.semaphore_wait(barrier, 40)

    def delivery(d, half):
        target = (owner + d) % 32
        columns = pl.ds(half * 16, 16)
        return pltpu.make_async_remote_copy(
            src_ref=features.at[target, :, columns], dst_ref=rows.at[pl.ds(owner * 2, 2), columns],
            send_sem=to_owner.at[half, target], recv_sem=at_owner.at[half, owner], **across(target)
        )

    def arrival(d, half):
        source = (owner + d) % 32
        columns = pl.ds(half * 16, 16)
        return pltpu.make_async_remote_copy(
            src_ref=features.at[source, :, columns], dst_ref=rows.at[pl.ds(source * 2, 2), columns],
            send_sem=to_owner.at[half, source], recv_sem=at_owner.at[half, source], **across(source)
        )

    for half in (1 - b0, b0):
        def deliver(d, carry):
            delivery(d, half).start()
            return carry

        lax.fori_loop(1, 32, deliver, 0)
    rows[pl.ds(owner * 2, 2)] = features[owner]

    def collect(half):
        def one(d, carry):
            arrival(d, half).wait_recv()
            return carry

        lax.fori_loop(1, 32, one, 0)
        leaf[pl.ds(half * 16, 16)] = jnp.transpose(rows[:, pl.ds(half * 16, 16)], (1, 0, 2))

    collect(1 - b0)

    leaf_copy = send(
        leaf.at[pl.ds((1 - b0) * 16, 16)], pair.at[:, pl.ds(b0 * 64, 64), :],
        bulk_send, bulk_recv, 0, 0, sister0,
    )
    collect(b0)

    def sent(d, carry):
        delivery(d, 0).wait_send()
        delivery(d, 1).wait_send()
        return carry

    lax.fori_loop(1, 32, sent, 0)

    def own_gram(r, acc):
        slab = leaf[r]
        return acc + bmm_nt(slab, slab)

    d_own = lax.fori_loop(0, 32, own_gram, jnp.zeros((64, 64), F32), unroll=8)
    d0_out[...] = pack(d_own)
    d_copy = send(d0_out, d0_in, small_send, small_recv, 0, 0, sister0)
    pair[:, pl.ds(b0 * 64, 64), :] = leaf[pl.ds(b0 * 16, 16)]

    early = []
    for other in range(2):
        target = sister1 - b0 + other
        offset = other * 16 + (1 - b1) * 8
        early.append((
            leaf.at[pl.ds(offset, 8)], quad.at[:, pl.ds(b0 * 64, 64), :],
            bulk_send, bulk_recv, 1 + other, 1 + b0, target,
        ))
    leaf_copy.wait()
    early = [send(*args) for args in early]
    d_copy.wait()

    def reduce_cross(partial, box, sems, recvs, members):
        mine = me % members
        base = me - mine
        box[mine] = pack(partial)
        copies = [
            send(box.at[mine], box.at[mine], sems, recvs, d, mine, base + (mine + d) % members)
            for d in range(1, members)
        ]
        for copy in copies:
            copy.wait_send()
        for d in range(1, members):
            source = (mine + d) % members
            pltpu.make_async_remote_copy(
                src_ref=box.at[source], dst_ref=box.at[source], send_sem=sems.at[d],
                recv_sem=recvs.at[source], **to(base + source)
            ).wait_recv()
        total = box[0]
        for i in range(1, members):
            total = total + box[i]
        return unpack(total)

    def cross0(r, acc):
        slab = pair[r]
        return acc + bmm_nt(slab[:64], slab[64:])

    cross = lax.fori_loop(0, 16, cross0, jnp.zeros((64, 64), F32), unroll=8)
    cross = reduce_cross(cross, x0, x0_send, x0_recv, 2)
    d_sister = unpack(d0_in[...])
    kernel = assemble(jnp.where(b0 == 0, d_own, d_sister), cross, jnp.where(b0 == 0, d_sister, d_own))
    basis, d_own = basis_of(kernel, start[...])
    qd_out[:64] = basis
    qd_out[64:] = pack(d_own)
    qd_copy = send(qd_out, qd_in, small_send, small_recv, 1, 1, sister1)

    def merged0(b, slabs, first, side):
        operand = jnp.concatenate(split3(b), axis=0)

        def one(r, carry):
            product = bmm(operand, slabs[first + r])
            product = product[:64] + product[64:128] + product[128:]
            hi, lo = split2(product)
            slab1[r, pl.ds(side * 128, 64), :] = hi
            slab1[r, pl.ds(side * 128 + 64, 64), :] = lo
            return carry

        lax.fori_loop(0, 8, one, 0, unroll=4)

    merged0(basis, pair, b1 * 8, b1)
    for copy in early:
        copy.wait_send()
    for other in range(2):
        pltpu.make_async_remote_copy(
            src_ref=leaf.at[pl.ds(0, 8)], dst_ref=quad.at[:, pl.ds(other * 64, 64), :],
            send_sem=bulk_send.at[1 + other], recv_sem=bulk_recv.at[1 + other], **to(sister1 - b0 + other)
        ).wait_recv()
    qd_copy.wait()
    merged0(qd_in[:64], quad, 0, 1 - b1)
    d_sister = unpack(qd_in[64:])

    def cross1(r, acc):
        slab = slab1[r]
        return acc + bmm_nt(slab[:128], slab[128:])

    acc = lax.fori_loop(0, 8, cross1, jnp.zeros((128, 128), F32), unroll=4)
    cross = acc[:64, :64] + acc[:64, 64:] + acc[64:, :64] + acc[64:, 64:]
    cross = reduce_cross(cross, x1, x1_send, x1_recv, 4)
    kernel = assemble(jnp.where(b1 == 0, d_own, d_sister), cross, jnp.where(b1 == 0, d_sister, d_own))
    basis, d_own = basis_of(kernel, start[...])
    d2_out[...] = pack(d_own)

    def merged(operand, slab):
        product = bmm(operand, slab)
        return product[:64] + product[64:]

    operand = split_basis(basis)
    for r in range(4):
        hi, lo = split2(merged(operand, slab1[(1 - b2) * 4 + r]))
        send2h[r] = hi
        send2l[r] = lo
    hi_copy = send(send2h, slab2.at[:, pl.ds(b2 * 128, 64), :], bulk_send, bulk_recv, 3, 3, sister2)
    d_copy = send(d2_out, d2_in, small_send, small_recv, 2, 2, sister2)
    for r in range(4):
        hi, lo = split2(merged(operand, slab1[b2 * 4 + r]))
        slab2[r, pl.ds(b2 * 128, 64), :] = hi
        slab2[r, pl.ds(b2 * 128 + 64, 64), :] = lo
    hi_copy.wait()
    d_copy.wait()
    d_sister = unpack(d2_in[...])
    cross = jnp.zeros((64, 64), F32)
    for r in range(4):
        cross = cross + bmm_nt(slab2[r, :64], slab2[r, 128:192])
    cross = reduce_cross(cross, x2, x2_send, x2_recv, 8)
    lo_copy = send(send2l, slab2.at[:, pl.ds(b2 * 128 + 64, 64), :], bulk_send, bulk_recv, 4, 4, sister2)
    kernel = assemble(jnp.where(b2 == 0, d_own, d_sister), cross, jnp.where(b2 == 0, d_sister, d_own))
    basis, _ = basis_of(kernel, start[...])
    lo_copy.wait()

    operand = split_basis(basis)
    column, side = me % 8, me // 8
    for r in range(4):
        hi, lo = split2(merged(operand, slab2[r]))
        slab3[column, r, pl.ds(side * 128, 64), :] = hi
        slab3[column, r, pl.ds(side * 128 + 64, 64), :] = lo

    def first_row(c):
        return (c % 2) * 16 + (c // 2 % 2) * 8 + (c // 4) * 4

    def add_along(index):
        index = index % 16
        c, upper = index % 8, index // 8
        total = along[upper]
        for r in range(4):
            total = total + bmm_nt(leaf[first_row(c) + r], slab3[c, r, pl.ds(upper * 128, 128), :])
        along[upper] = total

    def add_gram(c):
        total = wide[...]
        for r in range(4):
            slab = slab3[c, r]
            total = total + bmm_nt(slab, slab)
        wide[...] = total

    ring = Ring(me, slab3, ring_sems, to)
    along[...] = jnp.zeros_like(along)
    wide[...] = jnp.zeros_like(wide)
    ring.advance(1)
    add_along(me)
    for step in range(2, 10):
        ring.advance(step)
        distance = step - 1
        add_along(me + distance)
        if distance < 8:
            add_along(me + 16 - distance)
        if distance >= 4:
            add_gram((me + distance) % 8)
            if 4 < distance < 8:
                add_gram((me + 16 - distance) % 8)
    gram = wide[...]
    gram = jnp.concatenate([gram[:64] + gram[64:128], gram[128:192] + gram[192:]], axis=0)
    kernel = jnp.concatenate(
        [gram[:, :64] + gram[:, 64:128], gram[:, 128:192] + gram[:, 192:]], axis=1
    )
    basis, d_final = basis_of(kernel, start[...])

    row = lax.broadcasted_iota(jnp.int32, (64, 64), 0)
    col = lax.broadcasted_iota(jnp.int32, (64, 64), 1)
    eye = jnp.where(row == col, 1.0, 0.0)
    damping = 0.1 * jnp.sum(d_final * eye, keepdims=True) / 64 + 1e-06
    capacitance = d_final + damping * eye
    inverse = eliminate(capacitance, jnp.concatenate([eye, jnp.zeros((64, 64), F32)], axis=1))[:, :64]
    sides = [along[i][:, :64] + along[i][:, 64:] for i in range(2)]
    projected = mm_nt(jnp.concatenate(sides, axis=1), basis)
    weights = mm(mm_nt(projected, inverse), inverse)
    operand = split_basis(mm(weights, basis))

    def finish(c, carry):
        first = first_row(c)
        for r in range(0, 4, 2):
            one, two = [
                leaf[first + i].astype(F32)
                - merged(operand, slab3[c, i])
                for i in (r, r + 1)
            ]
            where = (first + r) // 2
            out[:, pl.ds(pl.multiple_of(where * 128, 128), 128)] = jnp.concatenate([one[:, :64], two[:, :64]], axis=1)
            out[:, pl.ds(pl.multiple_of((where + 16) * 128, 128), 128)] = jnp.concatenate([one[:, 64:], two[:, 64:]], axis=1)
        return carry

    lax.fori_loop(0, 8, finish, 0)
    ring.drain()


def per_device(tokens, lengths, module_order):
    dma = pltpu.SemaphoreType.DMA
    result = pl.pallas_call(
        tree_kernel,
        out_shape=jax.ShapeDtypeStruct((64, 4096), F32),
        in_specs=[pl.BlockSpec(memory_space=SMEM)] * 2 + [pl.BlockSpec(memory_space=VMEM)] * 2,
        out_specs=pl.BlockSpec(memory_space=VMEM),
        scratch_shapes=[
            pltpu.VMEM((32, 128, 128), BF16),
            pltpu.VMEM((32, 2, 32, 128), BF16),
            pltpu.VMEM((64, 32, 128), BF16),
            pltpu.VMEM((32, 64, 128), BF16),
            pltpu.VMEM((16, 128, 128), BF16),
            pltpu.VMEM((8, 128, 128), BF16),
            pltpu.VMEM((8, 256, 128), BF16),
            pltpu.VMEM((4, 256, 128), BF16),
            pltpu.VMEM((8, 4, 256, 128), BF16),
            pltpu.VMEM((4, 64, 128), BF16),
            pltpu.VMEM((4, 64, 128), BF16),
            pltpu.VMEM((2, 64, 128), F32),
            pltpu.VMEM((32, 128), F32),
            pltpu.VMEM((32, 128), F32),
            pltpu.VMEM((96, 128), F32),
            pltpu.VMEM((96, 128), F32),
            pltpu.VMEM((32, 128), F32),
            pltpu.VMEM((32, 128), F32),
            pltpu.VMEM((2, 32, 128), F32),
            pltpu.VMEM((4, 32, 128), F32),
            pltpu.VMEM((8, 32, 128), F32),
            pltpu.VMEM((256, 256), F32),
            dma((2, 32)), dma((2, 32)),
            dma((5,)), dma((5,)), dma((3,)), dma((3,)),
            dma((2,)), dma((2,)), dma((4,)), dma((4,)), dma((8,)), dma((8,)),
        ] + [dma((32,))] * 4,
        compiler_params=pltpu.CompilerParams(collective_id=0, has_side_effects=True),
        name="tree",
    )(lengths, module_order, tokens, jnp.asarray(start_rows(128, 64)))
    return result[None]


def solution(mesh):
    return jax.shard_map(
        per_device,
        mesh=mesh,
        in_specs=(P(("grp", "mod"), None, None, None), P(("grp", "mod")), P()),
        out_specs=P("mod", "grp", None),
        check_vma=False,
    )
```

```python
import functools

import jax
import jax.numpy as jnp
import numpy as np
from jax import lax
from jax.experimental import pallas as pl
from jax.experimental.pallas import tpu as pltpu
from jax.sharding import PartitionSpec as P

ITERS = 3
F32 = jnp.float32
BF16 = jnp.bfloat16
EXACT = lax.Precision.HIGHEST
VMEM = pltpu.MemorySpace.VMEM
SMEM = pltpu.MemorySpace.SMEM


def start_rows(row_count, col_count):
    row_index = np.arange(row_count, dtype=np.float64)[None, :] + 0.5
    col_index = np.arange(col_count, dtype=np.float64)[:, None] + 0.5
    return np.cos(np.pi * row_index * col_index / row_count).astype(np.float32)


def mm(a, b):
    return lax.dot_general(a, b, (((1,), (0,)), ((), ())), precision=EXACT, preferred_element_type=F32)


def mm_nt(a, b):
    return lax.dot_general(a, b, (((1,), (1,)), ((), ())), precision=EXACT, preferred_element_type=F32)


def bmm(a, b):
    return lax.dot_general(a, b, (((1,), (0,)), ((), ())), preferred_element_type=F32)


def bmm_nt(a, b):
    return lax.dot_general(a, b, (((1,), (1,)), ((), ())), preferred_element_type=F32)


def split2(x):
    hi = x.astype(BF16)
    return hi, (x - hi.astype(F32)).astype(BF16)


def split3(x):
    hi, rest = x.astype(BF16), None
    rest = x - hi.astype(F32)
    mid = rest.astype(BF16)
    return hi, mid, (rest - mid.astype(F32)).astype(BF16)


def eliminate(gram, rows):
    size = gram.shape[0]
    blocks = size // 8
    sub = lax.broadcasted_iota(jnp.int32, (8, 128), 0)
    padded = jnp.concatenate([gram, jnp.zeros((size, 128 - size), F32)], axis=1)
    left = [padded[8 * i : 8 * i + 8] for i in range(blocks)]
    right = [rows[8 * i : 8 * i + 8] for i in range(blocks)]

    def along_lanes(x, lane):
        return jnp.broadcast_to(x[:, lane : lane + 1], (8, 128))

    def along_rows(x, row):
        return jnp.broadcast_to(x[row : row + 1, :], (8, 128))

    done = []
    for k in range(blocks):
        p_left, p_right = left[k], right[k]
        cols = [along_lanes(p_left, 8 * k + c) for c in range(8)]
        below = {i: [along_lanes(left[i], 8 * k + c) for c in range(8)] for i in range(k + 1, blocks)}
        pivots = jnp.ones((8, 128), F32)
        reduced = jnp.zeros((8, 128), F32)
        for j in range(8):
            col = cols[j]
            pivot = along_rows(col, j)
            inverse = 1.0 / pivot
            here = sub == j
            pivots = jnp.where(here, pivot, pivots)
            row_right = along_rows(p_right, j)
            reduced = jnp.where(here, row_right, reduced)
            for c in range(j + 1, 8):
                scaled = along_rows(cols[c], j) * inverse
                cols[c] = jnp.where(here, scaled, cols[c] - col * scaled)
            scaled = along_rows(p_left, j) * inverse
            p_left = jnp.where(here, scaled, p_left - col * scaled)
            scaled = row_right * inverse
            p_right = jnp.where(here, scaled, p_right - col * scaled)
        done.append(reduced * lax.rsqrt(pivots))
        for c in range(8):
            row_left, row_right = along_rows(p_left, c), along_rows(p_right, c)
            for i in range(k + 1, blocks):
                left[i] = left[i] - below[i][c] * row_left
                right[i] = right[i] - below[i][c] * row_right
    return jnp.concatenate(done, axis=0)


def basis_of(kernel, start):
    def step(_, basis):
        image = mm(basis, kernel)
        return eliminate(mm_nt(image, image), image)

    basis = lax.fori_loop(0, ITERS, step, start)
    return basis, mm_nt(mm(basis, kernel), basis)


def pack(x):
    return jnp.concatenate([x[:32], x[32:]], axis=1)


def unpack(x):
    return jnp.concatenate([x[:, :64], x[:, 64:]], axis=0)


def assemble(lower, cross, upper):
    top = jnp.concatenate([lower, cross], axis=1)
    return jnp.concatenate([top, jnp.concatenate([cross.T, upper], axis=1)], axis=0)


def split_basis(basis):
    hi, lo = split2(basis)
    zero = jnp.zeros((64, 64), BF16)
    top = jnp.concatenate([hi[:, :64], hi[:, :64], hi[:, 64:], hi[:, 64:]], axis=1)
    low = jnp.concatenate([lo[:, :64], zero, lo[:, 64:], zero], axis=1)
    return jnp.concatenate([top, low], axis=0)


def features_of(x, live):
    zero = jnp.zeros((), x.dtype)
    x = jnp.where(live, x, zero)
    gradient = x.T[64:]
    lane = lax.broadcasted_iota(jnp.int32, gradient.shape, 1)
    sides = jnp.concatenate([jnp.where(lane < 64, gradient, zero), jnp.where(lane >= 64, gradient, zero)], axis=0)
    outer = bmm(sides, x)
    return [
        jnp.concatenate([outer[first : first + 32, :64], outer[first + 32 : first + 64, :64]], axis=1).astype(BF16)
        for first in (0, 64)
    ]


class Ring:
    def __init__(self, me, slabs, sems, to):
        self.me, self.slabs, self.to = me, slabs, to
        self.sems = {True: sems[:2], False: sems[2:]}

    def copy(self, distance, part, rightward, arriving):
        leg = 2 - distance % 2
        behind = distance if arriving else distance - leg
        origin = (self.me + 16 - behind if rightward else self.me + behind) % 16
        ref = self.slabs.at[origin % 8, part, pl.ds(origin // 8 * 64, 64), :]
        send, recv = self.sems[rightward]
        slot = (distance - 1) * 4 + part
        return pltpu.make_async_remote_copy(
            src_ref=ref, dst_ref=ref, send_sem=send.at[slot], recv_sem=recv.at[slot],
            **self.to((self.me + (leg if rightward else 16 - leg)) % 16)
        )

    @staticmethod
    def travels(distance, part, rightward):
        return distance < 8 or (part < 2) == rightward

    def advance(self, stage, part):
        for rightward in (True, False):
            if stage > 1 and self.travels(2 * stage - 2, part, rightward):
                self.copy(2 * stage - 2, part, rightward, True).wait_recv()
            for distance in (2 * stage, 2 * stage - 1):
                if stage < 5 and self.travels(distance, part, rightward):
                    self.copy(distance, part, rightward, False).start()

    def odd(self, stage, part):
        for rightward in (True, False):
            self.copy(2 * stage - 1, part, rightward, True).wait_recv()

    def drain(self):
        for distance in range(1, 9):
            for part in range(4):
                for rightward in (True, False):
                    if self.travels(distance, part, rightward):
                        self.copy(distance, part, rightward, False).wait_send()


def tree_kernel(
    lengths, order, tokens, start, out,
    by_module, features, rows, leaf,
    pair, quad, slab1, slab2, slab3, send2h, send2l, along,
    d0_out, d0_in, qd_out, qd_in, d2_out, d2_in,
    x0, x1, x2, wide,
    to_owner, at_owner,
    bulk_send, bulk_recv, small_send, small_recv,
    x0_send, x0_recv, x1_send, x1_recv, x2_send, x2_recv,
    *ring_sems,
):
    me, owner = lax.axis_index("grp"), lax.axis_index("mod")
    b0, b1, b2 = me % 2, (me // 2) % 2, (me // 4) % 2
    sister0 = me + 1 - 2 * b0
    sister1 = me + 2 - 4 * b1
    sister2 = me + 4 - 8 * b2

    def to(index):
        return dict(device_id={"grp": index}, device_id_type=pl.DeviceIdType.MESH)

    def across(index):
        return dict(device_id={"mod": index}, device_id_type=pl.DeviceIdType.MESH)

    def send(src, dst, sems, recvs, slot_send, slot_recv, index):
        copy = pltpu.make_async_remote_copy(
            src_ref=src, dst_ref=dst, send_sem=sems.at[slot_send], recv_sem=recvs.at[slot_recv], **to(index)
        )
        copy.start()
        return copy

    barrier = pltpu.get_barrier_semaphore()

    def greet(d, carry):
        pl.semaphore_signal(barrier, inc=1, **across((owner + d) % 32))
        return carry

    lax.fori_loop(1, 32, greet, 0)
    for d in range(1, 8):
        pl.semaphore_signal(barrier, inc=1, **to(me // 8 * 8 + (me + d) % 8))
    for d in (1, 2, 14, 15):
        pl.semaphore_signal(barrier, inc=1, **to((me + d) % 16))

    for example in range(2):
        by_module[:, pl.ds(example * 64, 64), :] = jnp.transpose(tokens[example], (1, 0, 2))
    token = lax.broadcasted_iota(jnp.int32, (128, 128), 0)
    live = token < jnp.where(token < 64, lengths[0], 64 + lengths[1])

    def make(group, carry):
        for i in range(16):
            slot = group * 16 + i
            first, second = features_of(by_module[order[slot]], live)
            features[slot, 0] = first
            features[slot, 1] = second
        return carry

    lax.fori_loop(0, 2, make, 0)
    pl.semaphore_wait(barrier, 42)

    def delivery(d, half):
        target = (owner + d) % 32
        columns = pl.ds(half * 16, 16)
        return pltpu.make_async_remote_copy(
            src_ref=features.at[target, :, columns], dst_ref=rows.at[pl.ds(owner * 2, 2), columns],
            send_sem=to_owner.at[half, target], recv_sem=at_owner.at[half, owner], **across(target)
        )

    def arrival(d, half):
        source = (owner + d) % 32
        columns = pl.ds(half * 16, 16)
        return pltpu.make_async_remote_copy(
            src_ref=features.at[source, :, columns], dst_ref=rows.at[pl.ds(source * 2, 2), columns],
            send_sem=to_owner.at[half, source], recv_sem=at_owner.at[half, source], **across(source)
        )

    for half in (1 - b0, b0):
        def deliver(d, carry):
            delivery(d, half).start()
            return carry

        lax.fori_loop(1, 32, deliver, 0)
    rows[pl.ds(owner * 2, 2)] = features[owner]

    def collect(half):
        def one(d, carry):
            arrival(d, half).wait_recv()
            return carry

        lax.fori_loop(1, 32, one, 0)
        leaf[pl.ds(half * 16, 16)] = jnp.transpose(rows[:, pl.ds(half * 16, 16)], (1, 0, 2))

    collect(1 - b0)

    leaf_copy = send(
        leaf.at[pl.ds((1 - b0) * 16, 16)], pair.at[:, pl.ds(b0 * 64, 64), :],
        bulk_send, bulk_recv, 0, 0, sister0,
    )
    collect(b0)

    def sent(d, carry):
        delivery(d, 0).wait_send()
        delivery(d, 1).wait_send()
        return carry

    lax.fori_loop(1, 32, sent, 0)

    def own_gram(r, acc):
        slab = leaf[r]
        return acc + bmm_nt(slab, slab)

    d_own = lax.fori_loop(0, 32, own_gram, jnp.zeros((64, 64), F32), unroll=8)
    d0_out[...] = pack(d_own)
    d_copy = send(d0_out, d0_in, small_send, small_recv, 0, 0, sister0)
    pair[:, pl.ds(b0 * 64, 64), :] = leaf[pl.ds(b0 * 16, 16)]

    early = []
    for other in range(2):
        target = sister1 - b0 + other
        offset = other * 16 + (1 - b1) * 8
        early.append((
            leaf.at[pl.ds(offset, 8)], quad.at[:, pl.ds(b0 * 64, 64), :],
            bulk_send, bulk_recv, 1 + other, 1 + b0, target,
        ))
    leaf_copy.wait()
    early = [send(*args) for args in early]
    d_copy.wait()

    def reduce_cross(partial, box, sems, recvs, members):
        mine = me % members
        base = me - mine
        box[mine] = pack(partial)
        copies = [
            send(box.at[mine], box.at[mine], sems, recvs, d, mine, base + (mine + d) % members)
            for d in range(1, members)
        ]
        for copy in copies:
            copy.wait_send()
        for d in range(1, members):
            source = (mine + d) % members
            pltpu.make_async_remote_copy(
                src_ref=box.at[source], dst_ref=box.at[source], send_sem=sems.at[d],
                recv_sem=recvs.at[source], **to(base + source)
            ).wait_recv()
        total = box[0]
        for i in range(1, members):
            total = total + box[i]
        return unpack(total)

    def cross0(r, acc):
        slab = pair[r]
        return acc + bmm_nt(slab[:64], slab[64:])

    cross = lax.fori_loop(0, 16, cross0, jnp.zeros((64, 64), F32), unroll=8)
    cross = reduce_cross(cross, x0, x0_send, x0_recv, 2)
    d_sister = unpack(d0_in[...])
    kernel = assemble(jnp.where(b0 == 0, d_own, d_sister), cross, jnp.where(b0 == 0, d_sister, d_own))
    basis, d_own = basis_of(kernel, start[...])
    qd_out[:64] = basis
    qd_out[64:] = pack(d_own)
    qd_copy = send(qd_out, qd_in, small_send, small_recv, 1, 1, sister1)

    def merged0(b, slabs, first, side):
        operand = jnp.concatenate(split3(b), axis=0)

        def one(r, carry):
            product = bmm(operand, slabs[first + r])
            product = product[:64] + product[64:128] + product[128:]
            hi, lo = split2(product)
            slab1[r, pl.ds(side * 128, 64), :] = hi
            slab1[r, pl.ds(side * 128 + 64, 64), :] = lo
            return carry

        lax.fori_loop(0, 8, one, 0, unroll=4)

    merged0(basis, pair, b1 * 8, b1)
    for copy in early:
        copy.wait_send()
    for other in range(2):
        pltpu.make_async_remote_copy(
            src_ref=leaf.at[pl.ds(0, 8)], dst_ref=quad.at[:, pl.ds(other * 64, 64), :],
            send_sem=bulk_send.at[1 + other], recv_sem=bulk_recv.at[1 + other], **to(sister1 - b0 + other)
        ).wait_recv()
    qd_copy.wait()
    merged0(qd_in[:64], quad, 0, 1 - b1)
    d_sister = unpack(qd_in[64:])

    def cross1(r, acc):
        slab = slab1[r]
        return acc + bmm_nt(slab[:128], slab[128:])

    acc = lax.fori_loop(0, 8, cross1, jnp.zeros((128, 128), F32), unroll=4)
    cross = acc[:64, :64] + acc[:64, 64:] + acc[64:, :64] + acc[64:, 64:]
    cross = reduce_cross(cross, x1, x1_send, x1_recv, 4)
    kernel = assemble(jnp.where(b1 == 0, d_own, d_sister), cross, jnp.where(b1 == 0, d_sister, d_own))
    basis, d_own = basis_of(kernel, start[...])
    d2_out[...] = pack(d_own)

    def merged(operand, slab):
        product = bmm(operand, slab)
        return product[:64] + product[64:]

    operand = split_basis(basis)
    for r in range(4):
        hi, lo = split2(merged(operand, slab1[(1 - b2) * 4 + r]))
        send2h[r] = hi
        send2l[r] = lo
    hi_copy = send(send2h, slab2.at[:, pl.ds(b2 * 128, 64), :], bulk_send, bulk_recv, 3, 3, sister2)
    d_copy = send(d2_out, d2_in, small_send, small_recv, 2, 2, sister2)
    for r in range(4):
        hi, lo = split2(merged(operand, slab1[b2 * 4 + r]))
        slab2[r, pl.ds(b2 * 128, 64), :] = hi
        slab2[r, pl.ds(b2 * 128 + 64, 64), :] = lo
    hi_copy.wait()
    d_copy.wait()
    d_sister = unpack(d2_in[...])
    cross = jnp.zeros((64, 64), F32)
    for r in range(4):
        cross = cross + bmm_nt(slab2[r, :64], slab2[r, 128:192])
    cross = reduce_cross(cross, x2, x2_send, x2_recv, 8)
    lo_copy = send(send2l, slab2.at[:, pl.ds(b2 * 128 + 64, 64), :], bulk_send, bulk_recv, 4, 4, sister2)
    kernel = assemble(jnp.where(b2 == 0, d_own, d_sister), cross, jnp.where(b2 == 0, d_sister, d_own))
    basis, _ = basis_of(kernel, start[...])
    lo_copy.wait()

    operand = split_basis(basis)
    column, side = me % 8, me // 8
    ring = Ring(me, slab3, ring_sems, to)
    for r in range(4):
        slab3[column, r, pl.ds(side * 64, 64), :] = merged(operand, slab2[r]).astype(BF16)
        ring.advance(1, r)

    def first_row(c):
        return (c % 2) * 16 + (c // 2 % 2) * 8 + (c // 4) * 4

    def add_along(index, r):
        index = index % 16
        c, upper = index % 8, index // 8
        along[upper] += bmm_nt(leaf[first_row(c) + r], slab3[c, r, pl.ds(upper * 64, 64), :])

    def add_gram(c, r):
        slab = slab3[c, r]
        wide[...] += bmm_nt(slab, slab)

    def take(distance, r):
        add_along(me + distance, r)
        if 0 < distance < 8:
            add_along(me + 16 - distance, r)
        if distance >= 4:
            add_gram((me + distance) % 8, r)
            if 4 < distance < 8:
                add_gram((me + 16 - distance) % 8, r)

    along[...] = jnp.zeros_like(along)
    wide[...] = jnp.zeros_like(wide)
    for stage in range(2, 6):
        for r in range(4):
            ring.advance(stage, r)
            ring.odd(stage - 1, r)
            if stage == 2:
                take(0, r)
            else:
                take(2 * stage - 5, r)
                take(2 * stage - 4, r)
    for r in range(4):
        take(7, r)
        take(8, r)
    kernel = wide[...]
    basis, d_final = basis_of(kernel, start[...])

    row = lax.broadcasted_iota(jnp.int32, (64, 64), 0)
    col = lax.broadcasted_iota(jnp.int32, (64, 64), 1)
    eye = jnp.where(row == col, 1.0, 0.0)
    damping = 0.1 * jnp.sum(d_final * eye, keepdims=True) / 64 + 1e-06
    capacitance = d_final + damping * eye
    inverse = eliminate(capacitance, jnp.concatenate([eye, jnp.zeros((64, 64), F32)], axis=1))[:, :64]
    projected = mm_nt(jnp.concatenate([along[0], along[1]], axis=1), basis)
    weights = mm(mm_nt(projected, inverse), inverse)
    operand = jnp.concatenate(split2(mm(weights, basis)), axis=0)

    def finish(c, carry):
        first = first_row(c)
        for r in range(0, 4, 2):
            one, two = [
                leaf[first + i].astype(F32)
                - merged(operand, slab3[c, i])
                for i in (r, r + 1)
            ]
            where = (first + r) // 2
            out[:, pl.ds(pl.multiple_of(where * 128, 128), 128)] = jnp.concatenate([one[:, :64], two[:, :64]], axis=1)
            out[:, pl.ds(pl.multiple_of((where + 16) * 128, 128), 128)] = jnp.concatenate([one[:, 64:], two[:, 64:]], axis=1)
        return carry

    lax.fori_loop(0, 8, finish, 0, unroll=4)
    ring.drain()


def per_device(tokens, lengths, module_order):
    dma = pltpu.SemaphoreType.DMA
    result = pl.pallas_call(
        tree_kernel,
        out_shape=jax.ShapeDtypeStruct((64, 4096), F32),
        in_specs=[pl.BlockSpec(memory_space=SMEM)] * 2 + [pl.BlockSpec(memory_space=VMEM)] * 2,
        out_specs=pl.BlockSpec(memory_space=VMEM),
        scratch_shapes=[
            pltpu.VMEM((32, 128, 128), BF16),
            pltpu.VMEM((32, 2, 32, 128), BF16),
            pltpu.VMEM((64, 32, 128), BF16),
            pltpu.VMEM((32, 64, 128), BF16),
            pltpu.VMEM((16, 128, 128), BF16),
            pltpu.VMEM((8, 128, 128), BF16),
            pltpu.VMEM((8, 256, 128), BF16),
            pltpu.VMEM((4, 256, 128), BF16),
            pltpu.VMEM((8, 4, 128, 128), BF16),
            pltpu.VMEM((4, 64, 128), BF16),
            pltpu.VMEM((4, 64, 128), BF16),
            pltpu.VMEM((2, 64, 64), F32),
            pltpu.VMEM((32, 128), F32),
            pltpu.VMEM((32, 128), F32),
            pltpu.VMEM((96, 128), F32),
            pltpu.VMEM((96, 128), F32),
            pltpu.VMEM((32, 128), F32),
            pltpu.VMEM((32, 128), F32),
            pltpu.VMEM((2, 32, 128), F32),
            pltpu.VMEM((4, 32, 128), F32),
            pltpu.VMEM((8, 32, 128), F32),
            pltpu.VMEM((128, 128), F32),
            dma((2, 32)), dma((2, 32)),
            dma((5,)), dma((5,)), dma((3,)), dma((3,)),
            dma((2,)), dma((2,)), dma((4,)), dma((4,)), dma((8,)), dma((8,)),
        ] + [dma((32,))] * 4,
        compiler_params=pltpu.CompilerParams(collective_id=0, has_side_effects=True),
        name="tree",
    )(lengths, module_order, tokens, jnp.asarray(start_rows(128, 64)))
    return result[None]


def solution(mesh):
    return jax.shard_map(
        per_device,
        mesh=mesh,
        in_specs=(P(("grp", "mod"), None, None, None), P(("grp", "mod")), P()),
        out_specs=P("mod", "grp", None),
        check_vma=False,
    )
```

```python
import functools

import jax
import jax.numpy as jnp
import numpy as np
from jax import lax
from jax.experimental import pallas as pl
from jax.experimental.pallas import tpu as pltpu
from jax.sharding import PartitionSpec as P

ITERS = 3
F32 = jnp.float32
BF16 = jnp.bfloat16
EXACT = lax.Precision.HIGHEST
VMEM = pltpu.MemorySpace.VMEM
SMEM = pltpu.MemorySpace.SMEM


def start_rows(row_count, col_count):
    row_index = np.arange(row_count, dtype=np.float64)[None, :] + 0.5
    col_index = np.arange(col_count, dtype=np.float64)[:, None] + 0.5
    return np.cos(np.pi * row_index * col_index / row_count).astype(np.float32)


def mm(a, b):
    return lax.dot_general(a, b, (((1,), (0,)), ((), ())), precision=EXACT, preferred_element_type=F32)


def mm_nt(a, b):
    return lax.dot_general(a, b, (((1,), (1,)), ((), ())), precision=EXACT, preferred_element_type=F32)


def bmm(a, b):
    return lax.dot_general(a, b, (((1,), (0,)), ((), ())), preferred_element_type=F32)


def bmm_nt(a, b):
    return lax.dot_general(a, b, (((1,), (1,)), ((), ())), preferred_element_type=F32)


def split2(x):
    hi = x.astype(BF16)
    return hi, (x - hi.astype(F32)).astype(BF16)


def split3(x):
    hi, rest = x.astype(BF16), None
    rest = x - hi.astype(F32)
    mid = rest.astype(BF16)
    return hi, mid, (rest - mid.astype(F32)).astype(BF16)


def eliminate(gram, rows):
    size = gram.shape[0]
    blocks = size // 8
    sub = lax.broadcasted_iota(jnp.int32, (8, 128), 0)
    padded = jnp.concatenate([gram, jnp.zeros((size, 128 - size), F32)], axis=1)
    left = [padded[8 * i : 8 * i + 8] for i in range(blocks)]
    right = [rows[8 * i : 8 * i + 8] for i in range(blocks)]

    def along_lanes(x, lane):
        return jnp.broadcast_to(x[:, lane : lane + 1], (8, 128))

    def along_rows(x, row):
        return jnp.broadcast_to(x[row : row + 1, :], (8, 128))

    done = []
    for k in range(blocks):
        cols = [along_lanes(left[k], 8 * k + c) for c in range(8)]
        below = {i: [along_lanes(left[i], 8 * k + c) for c in range(8)] for i in range(k + 1, blocks)}
        corner = {(r, c): along_rows(cols[c], r) for c in range(8) for r in range(c, 8)}
        row_left = [along_rows(left[k], r) for r in range(8)]
        row_right = [along_rows(right[k], r) for r in range(8)]
        pivots = jnp.ones((8, 128), F32)
        reduced = jnp.zeros((8, 128), F32)
        for j in range(8):
            inverse = 1.0 / corner[j, j]
            reduced = jnp.where(sub == j, row_right[j], reduced)
            pivots = jnp.where(sub == j, corner[j, j], pivots)
            factor = {r: corner[r, j] * inverse for r in range(j + 1, 8)}
            scaled_left, scaled_right = row_left[j] * inverse, row_right[j] * inverse
            for r in range(j + 1, 8):
                for c in range(j + 1, r + 1):
                    if c == r:
                        corner[r, c] = corner[r, c] - (corner[r, j] * corner[c, j]) * inverse
                    else:
                        corner[r, c] = corner[r, c] - factor[r] * corner[c, j]
                row_left[r] = row_left[r] - corner[r, j] * scaled_left
                row_right[r] = row_right[r] - corner[r, j] * scaled_right
            for i in range(k + 1, blocks):
                col = below[i][j]
                left[i] = left[i] - col * scaled_left
                right[i] = right[i] - col * scaled_right
                for c in range(j + 1, 8):
                    below[i][c] = below[i][c] - col * factor[c]
        done.append(reduced * lax.rsqrt(pivots))
    return jnp.concatenate(done, axis=0)


def basis_of(kernel, start):
    def step(_, basis):
        image = mm(basis, kernel)
        return eliminate(mm_nt(image, image), image)

    return lax.fori_loop(0, ITERS, step, start)


def gram_of(basis, kernel):
    return mm_nt(mm(basis, kernel), basis)


def pack(x):
    return jnp.concatenate([x[:32], x[32:]], axis=1)


def unpack(x):
    return jnp.concatenate([x[:, :64], x[:, 64:]], axis=0)


def assemble(lower, cross, upper):
    top = jnp.concatenate([lower, cross], axis=1)
    return jnp.concatenate([top, jnp.concatenate([cross.T, upper], axis=1)], axis=0)


def split_basis(basis):
    hi, lo = split2(basis)
    zero = jnp.zeros((64, 64), BF16)
    top = jnp.concatenate([hi[:, :64], hi[:, :64], hi[:, 64:], hi[:, 64:]], axis=1)
    low = jnp.concatenate([lo[:, :64], zero, lo[:, 64:], zero], axis=1)
    return jnp.concatenate([top, low], axis=0)


def features_of(x, live):
    zero = jnp.zeros((), x.dtype)
    x = jnp.where(live, x, zero)
    gradient = x.T[64:]
    lane = lax.broadcasted_iota(jnp.int32, gradient.shape, 1)
    sides = jnp.concatenate([jnp.where(lane < 64, gradient, zero), jnp.where(lane >= 64, gradient, zero)], axis=0)
    outer = bmm(sides, x)
    return [
        jnp.concatenate([outer[first : first + 32, :64], outer[first + 32 : first + 64, :64]], axis=1).astype(BF16)
        for first in (0, 64)
    ]


class Ring:
    def __init__(self, me, slabs, sems, to):
        self.me, self.slabs, self.to = me, slabs, to
        self.sems = {True: sems[:2], False: sems[2:]}

    def copy(self, distance, part, rightward, arriving):
        leg = 2 - distance % 2
        behind = distance if arriving else distance - leg
        origin = (self.me + 16 - behind if rightward else self.me + behind) % 16
        ref = self.slabs.at[origin % 8, part, pl.ds(origin // 8 * 64, 64), :]
        send, recv = self.sems[rightward]
        slot = (distance - 1) * 4 + part
        return pltpu.make_async_remote_copy(
            src_ref=ref, dst_ref=ref, send_sem=send.at[slot], recv_sem=recv.at[slot],
            **self.to((self.me + (leg if rightward else 16 - leg)) % 16)
        )

    @staticmethod
    def travels(distance, part, rightward):
        return distance < 8 or (part < 2) == rightward

    def advance(self, stage, part):
        for rightward in (True, False):
            if stage > 1 and self.travels(2 * stage - 2, part, rightward):
                self.copy(2 * stage - 2, part, rightward, True).wait_recv()
            for distance in (2 * stage, 2 * stage - 1):
                if stage < 5 and self.travels(distance, part, rightward):
                    self.copy(distance, part, rightward, False).start()

    def odd(self, stage, part):
        for rightward in (True, False):
            self.copy(2 * stage - 1, part, rightward, True).wait_recv()

    def drain(self):
        for distance in range(1, 9):
            for part in range(4):
                for rightward in (True, False):
                    if self.travels(distance, part, rightward):
                        self.copy(distance, part, rightward, False).wait_send()


def tree_kernel(
    lengths, order, tokens, start, out,
    by_module, features, rows, rows_over, leaf,
    pair, quad, slab1, slab2, slab3, send2h, send2l, along,
    d0_out, d0_in, qd_out, qd_in, d2_out, d2_in,
    x0, x1, x2, wide,
    to_owner, at_owner,
    bulk_send, bulk_recv, small_send, small_recv,
    x0_send, x0_recv, x1_send, x1_recv, x2_send, x2_recv,
    *ring_sems,
):
    me, owner = lax.axis_index("grp"), lax.axis_index("mod")
    b0, b1, b2 = me % 2, (me // 2) % 2, (me // 4) % 2
    sister0 = me + 1 - 2 * b0
    sister1 = me + 2 - 4 * b1
    sister2 = me + 4 - 8 * b2

    def to(index):
        return dict(device_id={"grp": index}, device_id_type=pl.DeviceIdType.MESH)

    def across(index):
        return dict(device_id={"mod": index}, device_id_type=pl.DeviceIdType.MESH)

    def send(src, dst, sems, recvs, slot_send, slot_recv, index):
        copy = pltpu.make_async_remote_copy(
            src_ref=src, dst_ref=dst, send_sem=sems.at[slot_send], recv_sem=recvs.at[slot_recv], **to(index)
        )
        copy.start()
        return copy

    def over(index):
        return dict(device_id={"grp": sister0, "mod": index}, device_id_type=pl.DeviceIdType.MESH)

    barrier = pltpu.get_barrier_semaphore()
    pl.semaphore_signal(barrier, inc=1, **over(owner))

    def greet(d, carry):
        target = (owner + d) % 32
        pl.semaphore_signal(barrier, inc=1, **across(target))
        pl.semaphore_signal(barrier, inc=1, **over(target))
        return carry

    lax.fori_loop(1, 32, greet, 0)
    for d in range(1, 8):
        pl.semaphore_signal(barrier, inc=1, **to(me // 8 * 8 + (me + d) % 8))
    for d in (1, 2, 14, 15):
        pl.semaphore_signal(barrier, inc=1, **to((me + d) % 16))

    for example in range(2):
        by_module[:, pl.ds(example * 64, 64), :] = jnp.transpose(tokens[example], (1, 0, 2))
    token = lax.broadcasted_iota(jnp.int32, (128, 128), 0)
    live = token < jnp.where(token < 64, lengths[0], 64 + lengths[1])

    def make(group, carry):
        for i in range(16):
            slot = group * 16 + i
            first, second = features_of(by_module[order[slot]], live)
            features[slot, 0] = first
            features[slot, 1] = second
        return carry

    lax.fori_loop(0, 2, make, 0)
    pl.semaphore_wait(barrier, 74)

    def delivery(d):
        target = (owner + d) % 32
        return pltpu.make_async_remote_copy(
            src_ref=features.at[target], dst_ref=rows.at[pl.ds(owner * 2, 2)],
            send_sem=to_owner.at[0, target], recv_sem=at_owner.at[0, owner], **across(target)
        )

    def arrival(d):
        source = (owner + d) % 32
        return pltpu.make_async_remote_copy(
            src_ref=features.at[source], dst_ref=rows.at[pl.ds(source * 2, 2)],
            send_sem=to_owner.at[0, source], recv_sem=at_owner.at[0, source], **across(source)
        )

    def delivery_over(d):
        target = (owner + d) % 32
        return pltpu.make_async_remote_copy(
            src_ref=features.at[target, :, pl.ds((1 - b0) * 16, 16)], dst_ref=rows_over.at[pl.ds(owner * 2, 2)],
            send_sem=to_owner.at[1, target], recv_sem=at_owner.at[1, owner], **over(target)
        )

    def arrival_over(d):
        source = (owner + d) % 32
        return pltpu.make_async_remote_copy(
            src_ref=features.at[source, :, pl.ds((1 - b0) * 16, 16)], dst_ref=rows_over.at[pl.ds(source * 2, 2)],
            send_sem=to_owner.at[1, source], recv_sem=at_owner.at[1, source], **over(source)
        )

    def deliver(d, carry):
        delivery_over(d).start()
        delivery(d).start()
        return carry

    lax.fori_loop(1, 32, deliver, 0)
    delivery_over(0).start()
    rows[pl.ds(owner * 2, 2)] = features[owner]

    def collect(d, carry):
        arrival(d).wait_recv()
        return carry

    lax.fori_loop(1, 32, collect, 0)
    leaf[...] = jnp.transpose(rows[...], (1, 0, 2))

    def own_gram(r, acc):
        slab = leaf[r]
        return acc + bmm_nt(slab, slab)

    d_own = lax.fori_loop(0, 32, own_gram, jnp.zeros((64, 64), F32), unroll=8)
    d0_out[...] = pack(d_own)
    d_copy = send(d0_out, d0_in, small_send, small_recv, 0, 0, sister0)
    early = []
    for other in range(2):
        target = sister1 - b0 + other
        offset = other * 16 + (1 - b1) * 8
        early.append(send(
            leaf.at[pl.ds(offset, 8)], quad.at[:, pl.ds(b0 * 64, 64), :],
            bulk_send, bulk_recv, 1 + other, 1 + b0, target,
        ))
    pair[:, pl.ds(b0 * 64, 64), :] = leaf[pl.ds(b0 * 16, 16)]

    def collect_over(d, carry):
        arrival_over(d).wait_recv()
        return carry

    lax.fori_loop(0, 32, collect_over, 0)
    pair[:, pl.ds((1 - b0) * 64, 64), :] = jnp.transpose(rows_over[...], (1, 0, 2))

    def reduce_cross(partial, box, sems, recvs, members):
        mine = me % members
        base = me - mine
        box[mine] = pack(partial)
        copies = [
            send(box.at[mine], box.at[mine], sems, recvs, d, mine, base + (mine + d) % members)
            for d in range(1, members)
        ]
        for copy in copies:
            copy.wait_send()
        for d in range(1, members):
            source = (mine + d) % members
            pltpu.make_async_remote_copy(
                src_ref=box.at[source], dst_ref=box.at[source], send_sem=sems.at[d],
                recv_sem=recvs.at[source], **to(base + source)
            ).wait_recv()
        total = box[0]
        for i in range(1, members):
            total = total + box[i]
        return unpack(total)

    def cross0(r, acc):
        slab = pair[r]
        return acc + bmm_nt(slab[:64], slab[64:])

    cross = lax.fori_loop(0, 16, cross0, jnp.zeros((64, 64), F32), unroll=8)
    cross = reduce_cross(cross, x0, x0_send, x0_recv, 2)
    d_copy.wait()

    def sent(d, carry):
        delivery(d).wait_send()
        delivery_over(d).wait_send()
        return carry

    lax.fori_loop(1, 32, sent, 0)
    delivery_over(0).wait_send()
    d_sister = unpack(d0_in[...])
    kernel = assemble(jnp.where(b0 == 0, d_own, d_sister), cross, jnp.where(b0 == 0, d_sister, d_own))
    basis = basis_of(kernel, start[...])
    qd_out[:64] = basis
    q_copy = send(qd_out.at[:64], qd_in.at[:64], small_send, small_recv, 1, 1, sister1)
    d_own = gram_of(basis, kernel)
    qd_out[64:] = pack(d_own)
    d_copy = send(qd_out.at[64:], qd_in.at[64:], small_send, small_recv, 3, 3, sister1)

    def merged0(b, slabs, first, side):
        operand = jnp.concatenate(split3(b), axis=0)

        def one(r, carry):
            product = bmm(operand, slabs[first + r])
            product = product[:64] + product[64:128] + product[128:]
            hi, lo = split2(product)
            slab1[r, pl.ds(side * 128, 64), :] = hi
            slab1[r, pl.ds(side * 128 + 64, 64), :] = lo
            return carry

        lax.fori_loop(0, 8, one, 0, unroll=4)

    merged0(basis, pair, b1 * 8, b1)
    for copy in early:
        copy.wait_send()
    for other in range(2):
        pltpu.make_async_remote_copy(
            src_ref=leaf.at[pl.ds(0, 8)], dst_ref=quad.at[:, pl.ds(other * 64, 64), :],
            send_sem=bulk_send.at[1 + other], recv_sem=bulk_recv.at[1 + other], **to(sister1 - b0 + other)
        ).wait_recv()
    q_copy.wait()
    merged0(qd_in[:64], quad, 0, 1 - b1)
    d_copy.wait()
    d_sister = unpack(qd_in[64:])

    def cross1(r, acc):
        slab = slab1[r]
        return acc + bmm_nt(slab[:128], slab[128:])

    acc = lax.fori_loop(0, 8, cross1, jnp.zeros((128, 128), F32), unroll=4)
    cross = acc[:64, :64] + acc[:64, 64:] + acc[64:, :64] + acc[64:, 64:]
    cross = reduce_cross(cross, x1, x1_send, x1_recv, 4)
    kernel = assemble(jnp.where(b1 == 0, d_own, d_sister), cross, jnp.where(b1 == 0, d_sister, d_own))
    basis = basis_of(kernel, start[...])

    def merged(operand, slab):
        product = bmm(operand, slab)
        return product[:64] + product[64:]

    operand = split_basis(basis)
    for r in range(4):
        hi, lo = split2(merged(operand, slab1[(1 - b2) * 4 + r]))
        send2h[r] = hi
        send2l[r] = lo
    hi_copy = send(send2h, slab2.at[:, pl.ds(b2 * 128, 64), :], bulk_send, bulk_recv, 3, 3, sister2)
    d_own = gram_of(basis, kernel)
    d2_out[...] = pack(d_own)
    d_copy = send(d2_out, d2_in, small_send, small_recv, 2, 2, sister2)
    for r in range(4):
        hi, lo = split2(merged(operand, slab1[b2 * 4 + r]))
        slab2[r, pl.ds(b2 * 128, 64), :] = hi
        slab2[r, pl.ds(b2 * 128 + 64, 64), :] = lo
    hi_copy.wait()
    d_copy.wait()
    d_sister = unpack(d2_in[...])
    cross = jnp.zeros((64, 64), F32)
    for r in range(4):
        cross = cross + bmm_nt(slab2[r, :64], slab2[r, 128:192])
    cross = reduce_cross(cross, x2, x2_send, x2_recv, 8)
    lo_copy = send(send2l, slab2.at[:, pl.ds(b2 * 128 + 64, 64), :], bulk_send, bulk_recv, 4, 4, sister2)
    kernel = assemble(jnp.where(b2 == 0, d_own, d_sister), cross, jnp.where(b2 == 0, d_sister, d_own))
    basis = basis_of(kernel, start[...])
    lo_copy.wait()

    operand = split_basis(basis)
    column, side = me % 8, me // 8
    ring = Ring(me, slab3, ring_sems, to)
    for r in range(4):
        slab3[column, r, pl.ds(side * 64, 64), :] = merged(operand, slab2[r]).astype(BF16)
        ring.advance(1, r)

    def first_row(c):
        return (c % 2) * 16 + (c // 2 % 2) * 8 + (c // 4) * 4

    def add_along(index, r):
        index = index % 16
        c, upper = index % 8, index // 8
        along[upper] += bmm_nt(leaf[first_row(c) + r], slab3[c, r, pl.ds(upper * 64, 64), :])

    def add_gram(c, r):
        slab = slab3[c, r]
        wide[...] += bmm_nt(slab, slab)

    def take(distance, r):
        add_along(me + distance, r)
        if 0 < distance < 8:
            add_along(me + 16 - distance, r)
        if distance >= 4:
            add_gram((me + distance) % 8, r)
            if 4 < distance < 8:
                add_gram((me + 16 - distance) % 8, r)

    along[...] = jnp.zeros_like(along)
    wide[...] = jnp.zeros_like(wide)
    for stage in range(2, 6):
        for r in range(4):
            ring.advance(stage, r)
            ring.odd(stage - 1, r)
            if stage == 2:
                take(0, r)
            else:
                take(2 * stage - 5, r)
                take(2 * stage - 4, r)
    for r in range(4):
        take(7, r)
        take(8, r)
    kernel = wide[...]
    basis = basis_of(kernel, start[...])
    d_final = gram_of(basis, kernel)

    row = lax.broadcasted_iota(jnp.int32, (64, 64), 0)
    col = lax.broadcasted_iota(jnp.int32, (64, 64), 1)
    eye = jnp.where(row == col, 1.0, 0.0)
    damping = 0.1 * jnp.sum(d_final * eye, keepdims=True) / 64 + 1e-06
    capacitance = d_final + damping * eye
    inverse = eliminate(capacitance, jnp.concatenate([eye, jnp.zeros((64, 64), F32)], axis=1))[:, :64]
    projected = mm_nt(jnp.concatenate([along[0], along[1]], axis=1), basis)
    weights = mm(mm_nt(projected, inverse), inverse)
    operand = jnp.concatenate(split2(mm(weights, basis)), axis=0)

    def finish(c, carry):
        first = first_row(c)
        for r in range(0, 4, 2):
            one, two = [
                leaf[first + i].astype(F32)
                - merged(operand, slab3[c, i])
                for i in (r, r + 1)
            ]
            where = (first + r) // 2
            out[:, pl.ds(pl.multiple_of(where * 128, 128), 128)] = jnp.concatenate([one[:, :64], two[:, :64]], axis=1)
            out[:, pl.ds(pl.multiple_of((where + 16) * 128, 128), 128)] = jnp.concatenate([one[:, 64:], two[:, 64:]], axis=1)
        return carry

    lax.fori_loop(0, 8, finish, 0, unroll=4)
    ring.drain()


def per_device(tokens, lengths, module_order):
    dma = pltpu.SemaphoreType.DMA
    result = pl.pallas_call(
        tree_kernel,
        out_shape=jax.ShapeDtypeStruct((64, 4096), F32),
        in_specs=[pl.BlockSpec(memory_space=SMEM)] * 2 + [pl.BlockSpec(memory_space=VMEM)] * 2,
        out_specs=pl.BlockSpec(memory_space=VMEM),
        scratch_shapes=[
            pltpu.VMEM((32, 128, 128), BF16),
            pltpu.VMEM((32, 2, 32, 128), BF16),
            pltpu.VMEM((64, 32, 128), BF16),
            pltpu.VMEM((64, 16, 128), BF16),
            pltpu.VMEM((32, 64, 128), BF16),
            pltpu.VMEM((16, 128, 128), BF16),
            pltpu.VMEM((8, 128, 128), BF16),
            pltpu.VMEM((8, 256, 128), BF16),
            pltpu.VMEM((4, 256, 128), BF16),
            pltpu.VMEM((8, 4, 128, 128), BF16),
            pltpu.VMEM((4, 64, 128), BF16),
            pltpu.VMEM((4, 64, 128), BF16),
            pltpu.VMEM((2, 64, 64), F32),
            pltpu.VMEM((32, 128), F32),
            pltpu.VMEM((32, 128), F32),
            pltpu.VMEM((96, 128), F32),
            pltpu.VMEM((96, 128), F32),
            pltpu.VMEM((32, 128), F32),
            pltpu.VMEM((32, 128), F32),
            pltpu.VMEM((2, 32, 128), F32),
            pltpu.VMEM((4, 32, 128), F32),
            pltpu.VMEM((8, 32, 128), F32),
            pltpu.VMEM((128, 128), F32),
            dma((2, 32)), dma((2, 32)),
            dma((5,)), dma((5,)), dma((4,)), dma((4,)),
            dma((2,)), dma((2,)), dma((4,)), dma((4,)), dma((8,)), dma((8,)),
        ] + [dma((32,))] * 4,
        compiler_params=pltpu.CompilerParams(collective_id=0, has_side_effects=True),
        name="tree",
    )(lengths, module_order, tokens, jnp.asarray(start_rows(128, 64)))
    return result[None]


def solution(mesh):
    return jax.shard_map(
        per_device,
        mesh=mesh,
        in_specs=(P(("grp", "mod"), None, None, None), P(("grp", "mod")), P()),
        out_specs=P("mod", "grp", None),
        check_vma=False,
    )
```
